768 devices in a mesh: tm: 48 (over y, z_hi, core), stripe: 16 (over z_lo, x).
Axes of the slice: x: 4, y: 8, z: 12 (z_hi: 3, z_lo: 4; z = z_hi * 4 + z_lo), core: 2. Of those that a mesh axis runs over, the one named last changes fastest.
Arguments:
- tokens: bfloat16 [96, 768, 1024], P('tm', 'stripe'), may hold values from -17 to 17, as said below
- time_input: bfloat16 [1024, 1536], replicated, may hold values from -0.1875 to 0.1875
- time_output: bfloat16 [512, 1024], replicated, may hold values from -0.25 to 0.25
- space_input: bfloat16 [1024, 1536], replicated, may hold values from -0.1875 to 0.1875
- space_output: bfloat16 [512, 1024], replicated, may hold values from -0.25 to 0.25
Outputs:
- encoded: bfloat16 [96, 768, 1024], P('tm', 'stripe')
The draws below stay inside these ranges and needn't reach their ends.
Inputs may be any that keep to these rules, and one draw needn't show every extreme that they name: Real-valued embeddings whose features and tokens have different scales.
All inputs are finite; a program needn't handle non-finite values.
Results may differ from the reference program's by a relative error of at most 0.01.
Values may be sent and summed in bfloat16 or wider, within the bound.
No kernel may reach another device: no remote copies, remote signals or barrier semaphores. Data moves between devices by JAX's collectives and lax.ppermute only.
A program may use at most 64 MiB of HBM per device.

```python
import math
import jax
import jax.numpy as jnp
from jax import lax

D = 1024
HEADS = 8
HEAD_DIM = 64
FRAMES = 96
PATCHES = 768


def draw_tokens(key, part):
    first, second, third = jax.random.split(key, 3)
    shape = (FRAMES, PATCHES, D)
    base = jax.random.truncated_normal(first, -3.0, 3.0, shape, jnp.float32)
    columns = jnp.exp(jax.random.uniform(second, (D,), jnp.float32, jnp.log(0.35), jnp.log(2.8)))
    rows = jnp.exp(jax.random.uniform(third, (FRAMES, PATCHES), jnp.float32, jnp.log(0.5), jnp.log(2.0)))
    return (base * rows[:, :, None] * columns[None, None, :]).astype(jnp.bfloat16)


def normal_values(rng, dims, deviation, limit, dtype=jnp.bfloat16):
    drawn = jax.random.normal(rng, dims, jnp.float32) * deviation
    return jnp.minimum(jnp.maximum(drawn, -limit), limit).astype(dtype)


def setup_inputs(seed: int = 0) -> dict:
    key_of = jax.random.split(jax.random.key(seed), 6)
    return {
        "tokens": draw_tokens(jax.random.fold_in(key_of[5], 71), 0),
        "time_input": normal_values(key_of[1], (D, HEADS * 3 * HEAD_DIM), D ** -0.5, 0.1875),
        "time_output": normal_values(key_of[2], (HEADS * HEAD_DIM, D), (HEADS * HEAD_DIM) ** -0.5, 0.25),
        "space_input": normal_values(key_of[3], (D, HEADS * 3 * HEAD_DIM), D ** -0.5, 0.1875),
        "space_output": normal_values(key_of[4], (HEADS * HEAD_DIM, D), (HEADS * HEAD_DIM) ** -0.5, 0.25),
    }


def layer_norm(values):
    wide = values.astype(jnp.float32)
    centre = lax.optimization_barrier(jnp.mean(wide, axis=-1, keepdims=True))
    spread = lax.optimization_barrier(jnp.mean((wide - centre) ** 2, axis=-1, keepdims=True))
    return ((wide - centre) * lax.rsqrt(spread + 1e-05)).astype(jnp.bfloat16)

def project(normed, weight):
    width = normed.shape[-1]
    lead = normed.shape[:-1]
    proj = jnp.dot(normed.reshape(-1, width), weight, preferred_element_type=jnp.float32)
    proj = proj.reshape(lead + (HEADS, 3, HEAD_DIM))
    query = proj[..., 0, :]
    key_part = proj[..., 1, :]
    query = query * lax.rsqrt(lax.optimization_barrier(jnp.mean(query * query, axis=-1, keepdims=True)) + 1e-06)
    key_part = key_part * lax.rsqrt(lax.optimization_barrier(jnp.mean(key_part * key_part, axis=-1, keepdims=True)) + 1e-06)
    return jnp.stack([query, key_part, proj[..., 2, :]], axis=-2).astype(jnp.bfloat16)

def attend(packed):
    query = packed[:, :, 0, :].astype(jnp.float32)
    key_part = packed[:, :, 1, :].astype(jnp.float32)
    value = packed[:, :, 2, :].astype(jnp.float32)
    scale = 2.0 / math.sqrt(HEAD_DIM)
    scores = jnp.einsum('qhc,khc->hqk', query, key_part) * scale
    weights = jnp.exp(scores)
    total = lax.optimization_barrier(jnp.sum(weights, axis=-1))
    rounded = lax.optimization_barrier(weights.astype(jnp.bfloat16)).astype(jnp.float32)
    summed = jnp.einsum('hqk,khc->qhc', rounded, value)
    return (summed / jnp.transpose(total)[:, :, None]).astype(jnp.bfloat16)

def reference(tokens, time_input, time_output, space_input, space_output):
    frames, patches, width = tokens.shape
    packed = project(layer_norm(tokens), time_input)
    by_patch = jnp.transpose(packed, (1, 0, 2, 3, 4))
    attn_time = lax.map(attend, by_patch)
    attn_time = jnp.transpose(attn_time, (1, 0, 2, 3)).reshape(frames * patches, HEADS * HEAD_DIM)
    mixed = tokens.astype(jnp.float32).reshape(frames * patches, width) + jnp.dot(attn_time, time_output, preferred_element_type=jnp.float32)
    hidden = mixed.astype(jnp.bfloat16).reshape(frames, patches, width)
    packed_space = project(layer_norm(hidden), space_input)
    attn_space = lax.map(attend, packed_space).reshape(frames * patches, HEADS * HEAD_DIM)
    final = hidden.astype(jnp.float32).reshape(frames * patches, width) + jnp.dot(attn_space, space_output, preferred_element_type=jnp.float32)
    return final.astype(jnp.bfloat16).reshape(frames, patches, width)
```

```python
import math

import jax
import jax.numpy as jnp
from jax import lax
from jax.sharding import PartitionSpec as P

HEAD_DIM = 64


def layer_norm(values):
    wide = values.astype(jnp.float32)
    centre = jnp.mean(wide, axis=-1, keepdims=True)
    spread = jnp.mean((wide - centre) ** 2, axis=-1, keepdims=True)
    return ((wide - centre) * lax.rsqrt(spread + 1e-05)).astype(jnp.bfloat16)


def normalize(proj):
    query = proj[..., 0, :]
    key_part = proj[..., 1, :]
    query = query * lax.rsqrt(jnp.mean(query * query, axis=-1, keepdims=True) + 1e-06)
    key_part = key_part * lax.rsqrt(jnp.mean(key_part * key_part, axis=-1, keepdims=True) + 1e-06)
    return (
        query.astype(jnp.bfloat16),
        key_part.astype(jnp.bfloat16),
        proj[..., 2, :].astype(jnp.bfloat16),
    )


def per_device(tokens, time_input, time_output, space_input, space_output):
    frames, patches, width = tokens.shape
    inner = time_output.shape[0]
    heads = inner // HEAD_DIM
    time_count = lax.axis_size("tm")
    stripe_count = lax.axis_size("stripe")
    scale = 2.0 / math.sqrt(HEAD_DIM)
    span = frames * time_count
    moved = lax.all_to_all(tokens, "tm", split_axis=1, concat_axis=0, tiled=True)
    moved = moved.reshape(span, width)
    proj = jnp.dot(layer_norm(moved), time_input, preferred_element_type=jnp.float32)
    query, key_part, value = normalize(proj.reshape(span, heads, 3, HEAD_DIM))
    scores = jnp.einsum("qhc,khc->hqk", query, key_part, preferred_element_type=jnp.float32)
    weights = jnp.exp(scores * scale)
    total = jnp.sum(weights, axis=-1)
    summed = jnp.einsum(
        "hqk,khc->qhc", weights.astype(jnp.bfloat16), value, preferred_element_type=jnp.float32
    )
    attn_time = (summed / jnp.transpose(total)[:, :, None]).astype(jnp.bfloat16)
    returned = lax.all_to_all(
        attn_time.reshape(span, 1, inner), "tm", split_axis=0, concat_axis=1, tiled=True
    )
    mixed = tokens.astype(jnp.float32).reshape(frames * patches, width) + jnp.dot(
        returned.reshape(frames * patches, inner), time_output, preferred_element_type=jnp.float32
    )
    hidden = mixed.astype(jnp.bfloat16)
    proj_space = jnp.dot(layer_norm(hidden), space_input, preferred_element_type=jnp.float32)
    packed = jnp.stack(
        normalize(proj_space.reshape(frames, patches, heads, 3, HEAD_DIM)), axis=3
    )
    packed = jnp.transpose(packed, (0, 2, 1, 3, 4)).reshape(
        frames * heads, patches, 3 * HEAD_DIM
    )
    pair = lax.all_to_all(packed, "stripe", split_axis=0, concat_axis=0, tiled=True)
    pair = pair.reshape(stripe_count * patches, 3 * HEAD_DIM)
    scores = jnp.dot(
        pair[:, :HEAD_DIM], pair[:, HEAD_DIM : 2 * HEAD_DIM].T, preferred_element_type=jnp.float32
    )
    weights = jnp.exp(scores * scale)
    total = jnp.sum(weights, axis=-1, keepdims=True)
    summed = jnp.dot(
        weights.astype(jnp.bfloat16), pair[:, 2 * HEAD_DIM :], preferred_element_type=jnp.float32
    )
    attn_space = (summed / total).astype(jnp.bfloat16)
    back = lax.all_to_all(
        attn_space.reshape(stripe_count, patches, HEAD_DIM),
        "stripe",
        split_axis=0,
        concat_axis=0,
        tiled=True,
    )
    back = jnp.transpose(back.reshape(frames, heads, patches, HEAD_DIM), (0, 2, 1, 3))
    branch = jnp.dot(
        back.reshape(frames * patches, inner), space_output, preferred_element_type=jnp.float32
    )
    final = hidden.astype(jnp.float32) + branch
    return final.astype(jnp.bfloat16).reshape(frames, patches, width)


def solution(mesh):
    placed = (P("tm", "stripe", None), P(), P(), P(), P())
    return jax.shard_map(
        per_device, mesh=mesh, in_specs=placed, out_specs=P("tm", "stripe", None), check_vma=False
    )
```

```python
import math

import jax
import jax.numpy as jnp
from jax import lax
from jax.experimental import pallas as pl
from jax.experimental.pallas import tpu as pltpu
from jax.sharding import PartitionSpec as P

HEAD_DIM = 64
LANES = 128
F32 = jnp.float32
BF16 = jnp.bfloat16
WEIGHT_SCALE = 2.0 / math.sqrt(HEAD_DIM) * math.log2(math.e)


def low_half(shape):
    return lax.broadcasted_iota(jnp.int32, shape, len(shape) - 1) < HEAD_DIM


def swap_halves(block):
    return pltpu.roll(block, HEAD_DIM, 1)


def layer_norm(wide):
    centre = jnp.mean(wide, axis=-1, keepdims=True)
    apart = wide - centre
    spread = jnp.mean(apart * apart, axis=-1, keepdims=True)
    return (apart * lax.rsqrt(spread + 1e-05)).astype(BF16)


def dot(left, right):
    return jnp.dot(left, right, preferred_element_type=F32)


def dot_t(left, right):
    return lax.dot_general(left, right, (((1,), (1,)), ((), ())), preferred_element_type=F32)


def packed_blocks(proj):
    rows, columns = proj.shape
    first = lax.broadcasted_iota(jnp.int32, (LANES, LANES), 0) // HEAD_DIM
    second = lax.broadcasted_iota(jnp.int32, (LANES, LANES), 1) // HEAD_DIM
    group = jnp.where(first == second, 1.0 / HEAD_DIM, 0.0).astype(BF16)
    low = low_half((rows, LANES))
    blocks = []
    for i in range(columns // LANES):
        block = proj[:, i * LANES : (i + 1) * LANES]
        square = block * block
        high = square.astype(BF16)
        rest = (square - high.astype(F32)).astype(BF16)
        factor = lax.rsqrt(dot(high, group) + dot(rest, group) + 1e-06)
        if i % 3 == 0:
            factor = jnp.where(low, factor * WEIGHT_SCALE, factor)
        elif i % 3 == 1:
            factor = jnp.where(low, 1.0, factor * WEIGHT_SCALE)
        else:
            factor = jnp.where(low, factor, 1.0)
        blocks.append(block * factor)
    return blocks


def send_tokens_kernel(tokens, out, rows):
    frames, patches, width = tokens.shape
    parts = width // LANES
    for f in range(frames):
        for c in range(parts):
            part = tokens[f, :, c * LANES : (c + 1) * LANES].astype(F32)
            rows[pl.ds(f * parts + c, patches, stride=frames * parts), :] = part
    out[...] = rows[...].reshape(out.shape).astype(BF16)


def time_kernel(tokens, weight, out, rows, sent):
    count, per, _ = tokens.shape
    width = weight.shape[0]
    parts = width // LANES
    span = count * per // parts
    rows[...] = tokens[...].astype(F32).reshape(rows.shape)
    wide = jnp.concatenate(
        [rows[pl.ds(c, span, stride=parts), :] for c in range(parts)], axis=1
    )
    blocks = packed_blocks(dot(layer_norm(wide), weight[...]))
    pairs = len(blocks) // 3
    low = low_half((span, LANES))
    for j in range(pairs):
        first, middle, last = blocks[3 * j : 3 * j + 3]
        mixed = jnp.where(low, last, middle)
        halves = []
        for query_key, is_low in ((first, True), (mixed, False)):
            keep = low if is_low else jnp.logical_not(low)
            query = jnp.where(keep, query_key, 0.0).astype(BF16)
            other = swap_halves(query_key).astype(BF16)
            weights = jnp.exp2(dot_t(query, other)).astype(BF16)
            value = jnp.where(keep, middle if is_low else last, 1.0).astype(BF16)
            halves.append(dot(weights, value))
        even, odd = halves
        total = swap_halves(jnp.where(low, odd, even))
        sent[pl.ds(j, span, stride=pairs), :] = jnp.where(low, even, odd) / total
    out[...] = sent[...].reshape(out.shape).astype(BF16)


def middle_kernel(attended, tokens, time_output, space_input, out, hidden_out, rows):
    frames, patches, width = tokens.shape
    inner = time_output.shape[0]
    parts = inner // LANES
    rows[...] = attended[...].astype(F32).reshape(rows.shape)
    back = jnp.concatenate(
        [
            jnp.concatenate(
                [
                    rows[pl.ds(f * parts + c, patches, stride=frames * parts), :]
                    for c in range(parts)
                ],
                axis=1,
            )
            for f in range(frames)
        ],
        axis=0,
    ).astype(BF16)
    wide = tokens[...].astype(F32).reshape(frames * patches, width)
    hidden = (wide + dot(back, time_output[...])).astype(BF16)
    hidden_out[...] = hidden
    blocks = packed_blocks(dot(layer_norm(hidden.astype(F32)), space_input[...]))
    pairs = len(blocks) // 3
    low = low_half((frames * patches, LANES))
    low_few = low_half((patches // 2, LANES))
    for j in range(pairs):
        first, middle, last = blocks[3 * j : 3 * j + 3]
        mixed = swap_halves(jnp.where(low, last, middle))
        for odd, query_key, value in ((0, first, middle), (1, mixed, last)):
            turned = swap_halves(value)
            lower, upper = (turned, value) if odd else (value, turned)
            for f in range(frames):
                start, half = f * patches, f * patches + patches // 2
                at = f * 2 * pairs + 2 * j + odd
                out[at, :patches, :] = query_key[start : start + patches].astype(BF16)
                out[at, patches:, :] = jnp.where(
                    low_few, lower[start:half], upper[half : start + patches]
                ).astype(BF16)


def space_kernel(pair, out):
    count, rows, _ = pair.shape
    half = rows // 3
    patches = 2 * half
    span = count * patches
    low = low_half((span, LANES))
    query_key = pair[:, :patches, :].reshape(span, LANES)
    wide = query_key.astype(F32)
    query = jnp.where(low, wide, 0.0).astype(BF16)
    keys = swap_halves(wide).astype(BF16)
    values = pair[:, patches:, :].astype(F32).reshape(count * half, LANES)
    turned = swap_halves(values)
    value = jnp.concatenate(
        [values.reshape(count, half, LANES), turned.reshape(count, half, LANES)], axis=1
    ).reshape(span, LANES)
    value = jnp.where(low, value, 1.0).astype(BF16)
    step = 4 * patches
    low_few = low_half((4, half, LANES))
    for i in range(span // step):
        weights = jnp.exp2(dot_t(query[i * step : (i + 1) * step], keys)).astype(BF16)
        summed = dot(weights, value)
        done = summed / swap_halves(summed)
        other = swap_halves(done).reshape(4, patches, LANES)
        done = done.reshape(4, patches, LANES)
        out[4 * i : 4 * i + 4] = jnp.where(low_few, done[:, :half], other[:, half:]).astype(BF16)


def final_kernel(back, hidden, weight, out):
    count, half, _ = back.shape
    frames, patches, width = out.shape
    heads = count // frames
    low = low_half((half, LANES))
    frame_rows = []
    for f in range(frames):
        columns = []
        for j in range(heads // 2):
            even = back[f * heads + 2 * j].astype(F32)
            odd = back[f * heads + 2 * j + 1].astype(F32)
            lower = jnp.where(low, even, swap_halves(odd))
            upper = jnp.where(low, swap_halves(even), odd)
            columns.append(jnp.concatenate([lower, upper], axis=0))
        frame_rows.append(jnp.concatenate(columns, axis=1))
    attended = jnp.concatenate(frame_rows, axis=0).astype(BF16)
    final = hidden[...].astype(F32) + dot(attended, weight[...])
    out[...] = final.astype(BF16).reshape(out.shape)


def call(kernel, out_shape, scratch, *args):
    return pl.pallas_call(
        kernel,
        out_shape=out_shape,
        in_specs=[pl.BlockSpec(memory_space=pltpu.VMEM)] * len(args),
        out_specs=jax.tree.map(lambda _: pl.BlockSpec(memory_space=pltpu.VMEM), out_shape),
        scratch_shapes=scratch,
    )(*args)


def array(*shape):
    return jax.ShapeDtypeStruct(shape, BF16)


def send_tokens(tokens):
    frames, patches, width = tokens.shape
    parts = width // LANES
    rows = pltpu.VMEM((frames * patches * parts, LANES), F32)
    return call(send_tokens_kernel, array(patches, frames * parts, LANES), [rows], tokens)


def time_half(moved, time_input):
    count, per, _ = moved.shape
    span = count * per * LANES // time_input.shape[0]
    parts = time_input.shape[1] // 3 // LANES
    rows = pltpu.VMEM((count * per, LANES), F32)
    sent = pltpu.VMEM((span * parts, LANES), F32)
    return call(
        time_kernel, array(count, span * parts // count, LANES), [rows, sent], moved, time_input
    )


def middle(returned, tokens, time_output, space_input):
    frames, patches, width = tokens.shape
    heads = time_output.shape[0] // HEAD_DIM
    count, per, _ = returned.shape
    rows = pltpu.VMEM((count * per, LANES), F32)
    shapes = (array(frames * heads, patches * 3 // 2, LANES), array(frames * patches, width))
    return call(middle_kernel, shapes, [rows], returned, tokens, time_output, space_input)


def space_half(pair):
    count, rows, _ = pair.shape
    return call(space_kernel, array(count, rows // 3, LANES), [], pair)


def final_half(back, hidden, space_output, shape):
    return call(final_kernel, array(*shape), [], back, hidden, space_output)


def per_device(tokens, time_input, time_output, space_input, space_output):
    moved = lax.all_to_all(send_tokens(tokens), "tm", 0, 0, tiled=True)
    attended = time_half(moved, time_input)
    returned = lax.all_to_all(attended, "tm", 0, 0, tiled=True)
    packed, hidden = middle(returned, tokens, time_output, space_input)
    pair = lax.all_to_all(packed, "stripe", 0, 0, tiled=True)
    back = lax.all_to_all(space_half(pair), "stripe", 0, 0, tiled=True)
    return final_half(back, hidden, space_output, tokens.shape)


def solution(mesh):
    placed = (P("tm", "stripe", None), P(), P(), P(), P())
    return jax.shard_map(
        per_device, mesh=mesh, in_specs=placed, out_specs=P("tm", "stripe", None), check_vma=False
    )
```

```python
import math

import jax
import jax.numpy as jnp
from jax import lax
from jax.experimental import pallas as pl
from jax.experimental.pallas import tpu as pltpu
from jax.sharding import PartitionSpec as P

HEAD_DIM = 64
LANES = 128
F32 = jnp.float32
BF16 = jnp.bfloat16
WEIGHT_SCALE = 2.0 / math.sqrt(HEAD_DIM) * math.log2(math.e)

COST = pl.CostEstimate(flops=2 * 10**9, transcendentals=0, bytes_accessed=2 * 10**7)


def low_half(shape):
    return lax.broadcasted_iota(jnp.int32, shape, len(shape) - 1) < HEAD_DIM


def swap_halves(block):
    return pltpu.roll(block, HEAD_DIM, 1)


def layer_norm(wide):
    centre = jnp.mean(wide, axis=-1, keepdims=True)
    apart = wide - centre
    spread = jnp.mean(apart * apart, axis=-1, keepdims=True)
    return (apart * lax.rsqrt(spread + 1e-05)).astype(BF16)


def dot(left, right):
    return jnp.dot(left, right, preferred_element_type=F32)


def dot_t(left, right):
    return lax.dot_general(left, right, (((1,), (1,)), ((), ())), preferred_element_type=F32)


def packed_blocks(proj):
    rows, columns = proj.shape
    first = lax.broadcasted_iota(jnp.int32, (LANES, LANES), 0) // HEAD_DIM
    second = lax.broadcasted_iota(jnp.int32, (LANES, LANES), 1) // HEAD_DIM
    group = jnp.where(first == second, 1.0 / HEAD_DIM, 0.0).astype(BF16)
    low = low_half((rows, LANES))
    blocks = []
    for i in range(columns // LANES):
        block = proj[:, i * LANES : (i + 1) * LANES]
        square = block * block
        high = square.astype(BF16)
        rest = (square - high.astype(F32)).astype(BF16)
        factor = lax.rsqrt(dot(high, group) + dot(rest, group) + 1e-06)
        if i % 3 == 0:
            factor = jnp.where(low, factor * WEIGHT_SCALE, factor)
        elif i % 3 == 1:
            factor = jnp.where(low, 1.0, factor * WEIGHT_SCALE)
        else:
            factor = jnp.where(low, factor, 1.0)
        blocks.append(block * factor)
    return blocks


def send_tokens_kernel(tokens, out, rows):
    frames, patches, width = tokens.shape
    parts = width // LANES
    for f in range(frames):
        for c in range(parts):
            part = tokens[f, :, c * LANES : (c + 1) * LANES].astype(F32)
            rows[pl.ds(f * parts + c, patches, stride=frames * parts), :] = part
    out[...] = rows[...].reshape(out.shape).astype(BF16)


def time_kernel(tokens, weight, out, rows, sent):
    count, per, _ = tokens.shape
    width = weight.shape[0]
    parts = width // LANES
    span = count * per // parts
    rows[...] = tokens[...].astype(F32).reshape(rows.shape)
    wide = jnp.concatenate(
        [rows[pl.ds(c, span, stride=parts), :] for c in range(parts)], axis=1
    )
    blocks = packed_blocks(dot(layer_norm(wide), weight[...]))
    pairs = len(blocks) // 3
    low = low_half((span, LANES))
    for j in range(pairs):
        first, middle, last = blocks[3 * j : 3 * j + 3]
        mixed = jnp.where(low, last, middle)
        halves = []
        for query_key, is_low in ((first, True), (mixed, False)):
            keep = low if is_low else jnp.logical_not(low)
            query = jnp.where(keep, query_key, 0.0).astype(BF16)
            other = swap_halves(query_key).astype(BF16)
            weights = jnp.exp2(dot_t(query, other)).astype(BF16)
            value = jnp.where(keep, middle if is_low else last, 1.0).astype(BF16)
            halves.append(dot(weights, value))
        even, odd = halves
        total = swap_halves(jnp.where(low, odd, even))
        sent[pl.ds(j, span, stride=pairs), :] = jnp.where(low, even, odd) / total
    out[...] = sent[...].reshape(out.shape).astype(BF16)


def middle_kernel(attended, tokens, time_output, space_input, out, hidden_out, rows):
    frames, patches, width = tokens.shape
    inner = time_output.shape[0]
    parts = inner // LANES
    rows[...] = attended[...].astype(F32).reshape(rows.shape)
    back = jnp.concatenate(
        [
            jnp.concatenate(
                [
                    rows[pl.ds(f * parts + c, patches, stride=frames * parts), :]
                    for c in range(parts)
                ],
                axis=1,
            )
            for f in range(frames)
        ],
        axis=0,
    ).astype(BF16)
    wide = tokens[...].astype(F32).reshape(frames * patches, width)
    hidden = (wide + dot(back, time_output[...])).astype(BF16)
    hidden_out[...] = hidden
    blocks = packed_blocks(dot(layer_norm(hidden.astype(F32)), space_input[...]))
    pairs = len(blocks) // 3
    low = low_half((frames * patches, LANES))
    low_few = low_half((patches // 2, LANES))
    for j in range(pairs):
        first, middle, last = blocks[3 * j : 3 * j + 3]
        mixed = swap_halves(jnp.where(low, last, middle))
        for odd, query_key, value in ((0, first, middle), (1, mixed, last)):
            turned = swap_halves(value)
            lower, upper = (turned, value) if odd else (value, turned)
            for f in range(frames):
                start, half = f * patches, f * patches + patches // 2
                at = f * 2 * pairs + 2 * j + odd
                out[at, :patches, :] = query_key[start : start + patches].astype(BF16)
                out[at, patches:, :] = jnp.where(
                    low_few, lower[start:half], upper[half : start + patches]
                ).astype(BF16)


def space_kernel(pair, out):
    count, rows, _ = pair.shape
    half = rows // 3
    patches = 2 * half
    span = count * patches
    low = low_half((span, LANES))
    query_key = pair[:, :patches, :].reshape(span, LANES)
    wide = query_key.astype(F32)
    query = jnp.where(low, wide, 0.0).astype(BF16)
    keys = swap_halves(wide).astype(BF16)
    values = pair[:, patches:, :].astype(F32).reshape(count * half, LANES)
    turned = swap_halves(values)
    value = jnp.concatenate(
        [values.reshape(count, half, LANES), turned.reshape(count, half, LANES)], axis=1
    ).reshape(span, LANES)
    value = jnp.where(low, value, 1.0).astype(BF16)
    step = 4 * patches
    low_few = low_half((4, half, LANES))
    for i in range(span // step):
        weights = jnp.exp2(dot_t(query[i * step : (i + 1) * step], keys)).astype(BF16)
        summed = dot(weights, value)
        done = summed / swap_halves(summed)
        other = swap_halves(done).reshape(4, patches, LANES)
        done = done.reshape(4, patches, LANES)
        out[4 * i : 4 * i + 4] = jnp.where(low_few, done[:, :half], other[:, half:]).astype(BF16)


def final_kernel(back, hidden, weight, out):
    count, half, _ = back.shape
    frames, patches, width = out.shape
    heads = count // frames
    low = low_half((half, LANES))
    frame_rows = []
    for f in range(frames):
        columns = []
        for j in range(heads // 2):
            even = back[f * heads + 2 * j].astype(F32)
            odd = back[f * heads + 2 * j + 1].astype(F32)
            lower = jnp.where(low, even, swap_halves(odd))
            upper = jnp.where(low, swap_halves(even), odd)
            columns.append(jnp.concatenate([lower, upper], axis=0))
        frame_rows.append(jnp.concatenate(columns, axis=1))
    attended = jnp.concatenate(frame_rows, axis=0).astype(BF16)
    final = hidden[...].astype(F32) + dot(attended, weight[...])
    out[...] = final.astype(BF16).reshape(out.shape)


def call(kernel, out_shape, scratch, *args, cost=None):
    return pl.pallas_call(
        kernel,
        out_shape=out_shape,
        in_specs=[pl.BlockSpec(memory_space=pltpu.VMEM)] * len(args),
        out_specs=jax.tree.map(lambda _: pl.BlockSpec(memory_space=pltpu.VMEM), out_shape),
        scratch_shapes=scratch,
        compiler_params=pltpu.CompilerParams(vmem_limit_bytes=12 * 2**20),
        cost_estimate=cost,
    )(*[pltpu.with_memory_space_constraint(arg, pltpu.VMEM) for arg in args])


def array(*shape):
    return pltpu.VMEM(shape, BF16)


def send_tokens(tokens):
    frames, patches, width = tokens.shape
    parts = width // LANES
    rows = pltpu.VMEM((frames * patches * parts, LANES), F32)
    return call(send_tokens_kernel, array(patches, frames * parts, LANES), [rows], tokens, cost=COST)


def time_half(moved, time_input):
    count, per, _ = moved.shape
    span = count * per * LANES // time_input.shape[0]
    parts = time_input.shape[1] // 3 // LANES
    rows = pltpu.VMEM((count * per, LANES), F32)
    sent = pltpu.VMEM((span * parts, LANES), F32)
    return call(
        time_kernel, array(count, span * parts // count, LANES), [rows, sent], moved, time_input
    )


def middle(returned, tokens, time_output, space_input):
    frames, patches, width = tokens.shape
    heads = time_output.shape[0] // HEAD_DIM
    count, per, _ = returned.shape
    rows = pltpu.VMEM((count * per, LANES), F32)
    shapes = (array(frames * heads, patches * 3 // 2, LANES), array(frames * patches, width))
    return call(middle_kernel, shapes, [rows], returned, tokens, time_output, space_input)


def space_half(pair):
    count, rows, _ = pair.shape
    return call(space_kernel, array(count, rows // 3, LANES), [], pair)


def final_half(back, hidden, space_output, shape):
    return call(final_kernel, jax.ShapeDtypeStruct(shape, BF16), [], back, hidden, space_output)


def per_device(tokens, time_input, time_output, space_input, space_output):
    moved = lax.all_to_all(send_tokens(tokens), "tm", 0, 0, tiled=True)
    attended = time_half(moved, time_input)
    returned = lax.all_to_all(attended, "tm", 0, 0, tiled=True)
    packed, hidden = middle(returned, tokens, time_output, space_input)
    pair = lax.all_to_all(packed, "stripe", 0, 0, tiled=True)
    back = lax.all_to_all(space_half(pair), "stripe", 0, 0, tiled=True)
    return final_half(back, hidden, space_output, tokens.shape)


def solution(mesh):
    placed = (P("tm", "stripe", None), P(), P(), P(), P())
    return jax.shard_map(
        per_device, mesh=mesh, in_specs=placed, out_specs=P("tm", "stripe", None), check_vma=False
    )
```

```python
import math

import jax
import jax.numpy as jnp
from jax import lax
from jax.experimental import pallas as pl
from jax.experimental.pallas import tpu as pltpu
from jax.sharding import PartitionSpec as P

HEAD_DIM = 64
LANES = 128
F32 = jnp.float32
BF16 = jnp.bfloat16
WEIGHT_SCALE = 2.0 / math.sqrt(HEAD_DIM) * math.log2(math.e)

AHEAD = pl.CostEstimate(flops=5 * 10**9, transcendentals=0, bytes_accessed=4 * 10**5)


def low_half(shape):
    return lax.broadcasted_iota(jnp.int32, shape, len(shape) - 1) < HEAD_DIM


def swap_halves(block):
    return pltpu.roll(block, HEAD_DIM, 1)


def layer_norm(wide):
    centre = jnp.mean(wide, axis=-1, keepdims=True)
    apart = wide - centre
    spread = jnp.mean(apart * apart, axis=-1, keepdims=True)
    return (apart * lax.rsqrt(spread + 1e-05)).astype(BF16)


def dot(left, right):
    return jnp.dot(left, right, preferred_element_type=F32)


def dot_t(left, right):
    return lax.dot_general(left, right, (((1,), (1,)), ((), ())), preferred_element_type=F32)


def packed_blocks(proj):
    rows, columns = proj.shape
    first = lax.broadcasted_iota(jnp.int32, (2 * LANES, LANES), 0) // HEAD_DIM % 2
    second = lax.broadcasted_iota(jnp.int32, (2 * LANES, LANES), 1) // HEAD_DIM
    group = jnp.where(first == second, 1.0 / HEAD_DIM, 0.0).astype(BF16)
    low = low_half((rows, LANES))
    parts = [proj[:, i * LANES : (i + 1) * LANES] for i in range(columns // LANES)]
    means = []
    for part in parts:
        square = part * part
        high = square.astype(BF16)
        rest = (square - high.astype(F32)).astype(BF16)
        means.append(dot(jnp.concatenate([high, rest], axis=1), group))
    blocks = []
    for i, (part, mean) in enumerate(zip(parts, means, strict=True)):
        factor = lax.rsqrt(mean + 1e-06)
        if i % 3 == 0:
            factor = jnp.where(low, factor * WEIGHT_SCALE, factor)
        elif i % 3 == 1:
            factor = jnp.where(low, 1.0, factor * WEIGHT_SCALE)
        else:
            factor = jnp.where(low, factor, 1.0)
        blocks.append(part * factor)
    return blocks


def send_tokens_kernel(tokens, out, rows):
    frames, patches, width = tokens.shape
    parts = width // LANES
    for f in range(frames):
        for c in range(parts):
            part = tokens[f, :, c * LANES : (c + 1) * LANES].astype(F32)
            rows[pl.ds(f * parts + c, patches, stride=frames * parts), :] = part
    out[...] = rows[...].reshape(out.shape).astype(BF16)


def time_kernel(tokens, weight, out, rows, sent):
    count, per, _ = tokens.shape
    width = weight.shape[0]
    parts = width // LANES
    span = count * per // parts
    rows[...] = tokens[...].astype(F32).reshape(rows.shape)
    wide = jnp.concatenate(
        [rows[pl.ds(c, span, stride=parts), :] for c in range(parts)], axis=1
    )
    blocks = packed_blocks(dot(layer_norm(wide), weight[...]))
    pairs = len(blocks) // 3
    low = low_half((span, LANES))
    high = jnp.logical_not(low)
    heads = []
    for j in range(pairs):
        first, middle, last = blocks[3 * j : 3 * j + 3]
        heads.append((low, first, middle))
        heads.append((high, jnp.where(low, last, middle), last))
    scores = [
        dot_t(jnp.where(keep, both, 0.0).astype(BF16), swap_halves(both).astype(BF16))
        for keep, both, _ in heads
    ]
    weights = [jnp.exp2(score).astype(BF16) for score in scores]
    summed = [
        dot(weight, jnp.where(keep, block, 1.0).astype(BF16))
        for weight, (keep, _, block) in zip(weights, heads, strict=True)
    ]
    for j in range(pairs):
        even, odd = summed[2 * j : 2 * j + 2]
        total = swap_halves(jnp.where(low, odd, even))
        sent[pl.ds(j, span, stride=pairs), :] = jnp.where(low, even, odd) / total
    out[...] = sent[...].reshape(out.shape).astype(BF16)


def middle_kernel(attended, tokens, time_output, space_input, out, hidden_out, rows):
    frames, patches, width = tokens.shape
    inner = time_output.shape[0]
    parts = inner // LANES
    rows[...] = attended[...].astype(F32).reshape(rows.shape)
    back = jnp.concatenate(
        [
            jnp.concatenate(
                [
                    rows[pl.ds(f * parts + c, patches, stride=frames * parts), :]
                    for c in range(parts)
                ],
                axis=1,
            )
            for f in range(frames)
        ],
        axis=0,
    ).astype(BF16)
    wide = tokens[...].astype(F32).reshape(frames * patches, width)
    hidden = (wide + dot(back, time_output[...])).astype(BF16)
    hidden_out[...] = hidden
    blocks = packed_blocks(dot(layer_norm(hidden.astype(F32)), space_input[...]))
    pairs = len(blocks) // 3
    low = low_half((frames * patches, LANES))
    low_few = low_half((patches // 2, LANES))
    for j in range(pairs):
        first, middle, last = blocks[3 * j : 3 * j + 3]
        mixed = swap_halves(jnp.where(low, last, middle))
        for odd, query_key, value in ((0, first, middle), (1, mixed, last)):
            turned = swap_halves(value)
            lower, upper = (turned, value) if odd else (value, turned)
            for f in range(frames):
                start, half = f * patches, f * patches + patches // 2
                at = f * 2 * pairs + 2 * j + odd
                out[at, :patches, :] = query_key[start : start + patches].astype(BF16)
                out[at, patches:, :] = jnp.where(
                    low_few, lower[start:half], upper[half : start + patches]
                ).astype(BF16)


def space_kernel(pair, out):
    count, rows, _ = pair.shape
    half = rows // 3
    patches = 2 * half
    span = count * patches
    low = low_half((span, LANES))
    query_key = pair[:, :patches, :].reshape(span, LANES)
    wide = query_key.astype(F32)
    query = jnp.where(low, wide, 0.0).astype(BF16)
    keys = swap_halves(wide).astype(BF16)
    values = pair[:, patches:, :].astype(F32).reshape(count * half, LANES)
    turned = swap_halves(values)
    value = jnp.concatenate(
        [values.reshape(count, half, LANES), turned.reshape(count, half, LANES)], axis=1
    ).reshape(span, LANES)
    value = jnp.where(low, value, 1.0).astype(BF16)
    weights = jnp.exp2(dot_t(query, keys)).astype(BF16)
    summed = dot(weights, value)
    done = summed / swap_halves(summed)
    other = swap_halves(done).reshape(count, patches, LANES)
    done = done.reshape(count, patches, LANES)
    low_few = low_half((count, half, LANES))
    out[...] = jnp.where(low_few, done[:, :half], other[:, half:]).astype(BF16)


def final_kernel(back, hidden, weight, out):
    count, half, _ = back.shape
    frames, patches, width = out.shape
    heads = count // frames
    low = low_half((half, LANES))
    frame_rows = []
    for f in range(frames):
        columns = []
        for j in range(heads // 2):
            even = back[f * heads + 2 * j].astype(F32)
            odd = back[f * heads + 2 * j + 1].astype(F32)
            lower = jnp.where(low, even, swap_halves(odd))
            upper = jnp.where(low, swap_halves(even), odd)
            columns.append(jnp.concatenate([lower, upper], axis=0))
        frame_rows.append(jnp.concatenate(columns, axis=1))
    attended = jnp.concatenate(frame_rows, axis=0).astype(BF16)
    final = hidden[...].astype(F32) + dot(attended, weight[...])
    out[...] = final.astype(BF16).reshape(out.shape)


def call(kernel, out_shape, scratch, *args, cost=None):
    return pl.pallas_call(
        kernel,
        out_shape=out_shape,
        in_specs=[pl.BlockSpec(memory_space=pltpu.VMEM)] * len(args),
        out_specs=jax.tree.map(lambda _: pl.BlockSpec(memory_space=pltpu.VMEM), out_shape),
        scratch_shapes=scratch,
        compiler_params=pltpu.CompilerParams(vmem_limit_bytes=12 * 2**20),
        cost_estimate=cost,
    )(*[pltpu.with_memory_space_constraint(arg, pltpu.VMEM) for arg in args])


def array(*shape):
    return pltpu.VMEM(shape, BF16)


def send_tokens(tokens):
    frames, patches, width = tokens.shape
    parts = width // LANES
    rows = pltpu.VMEM((frames * patches * parts, LANES), F32)
    return call(send_tokens_kernel, array(patches, frames * parts, LANES), [rows], tokens, cost=AHEAD)


def time_half(moved, time_input):
    count, per, _ = moved.shape
    span = count * per * LANES // time_input.shape[0]
    parts = time_input.shape[1] // 3 // LANES
    rows = pltpu.VMEM((count * per, LANES), F32)
    sent = pltpu.VMEM((span * parts, LANES), F32)
    shape = array(count, span * parts // count, LANES)
    return call(time_kernel, shape, [rows, sent], moved, time_input, cost=AHEAD)


def middle(returned, tokens, time_output, space_input):
    frames, patches, width = tokens.shape
    heads = time_output.shape[0] // HEAD_DIM
    count, per, _ = returned.shape
    rows = pltpu.VMEM((count * per, LANES), F32)
    shapes = (array(frames * heads, patches * 3 // 2, LANES), array(frames * patches, width))
    return call(middle_kernel, shapes, [rows], returned, tokens, time_output, space_input)


def space_half(pair):
    count, rows, _ = pair.shape
    return call(space_kernel, array(count, rows // 3, LANES), [], pair)


def final_half(back, hidden, space_output, shape):
    return call(final_kernel, jax.ShapeDtypeStruct(shape, BF16), [], back, hidden, space_output)


def per_device(tokens, time_input, time_output, space_input, space_output):
    moved = lax.all_to_all(send_tokens(tokens), "tm", 0, 0, tiled=True)
    attended = time_half(moved, time_input)
    returned = lax.all_to_all(attended, "tm", 0, 0, tiled=True)
    packed, hidden = middle(returned, tokens, time_output, space_input)
    pair = lax.all_to_all(packed, "stripe", 0, 0, tiled=True)
    back = lax.all_to_all(space_half(pair), "stripe", 0, 0, tiled=True)
    return final_half(back, hidden, space_output, tokens.shape)


def solution(mesh):
    placed = (P("tm", "stripe", None), P(), P(), P(), P())
    return jax.shard_map(
        per_device, mesh=mesh, in_specs=placed, out_specs=P("tm", "stripe", None), check_vma=False
    )
```

```python
import math

import jax
import jax.numpy as jnp
from jax import lax
from jax.experimental import pallas as pl
from jax.experimental.pallas import tpu as pltpu
from jax.sharding import PartitionSpec as P

HEAD_DIM = 64
LANES = 128
F32 = jnp.float32
BF16 = jnp.bfloat16
WEIGHT_SCALE = 2.0 / math.sqrt(HEAD_DIM) * math.log2(math.e)

TIME_FIRST = 28
AHEAD = pl.CostEstimate(flops=5 * 10**9, transcendentals=0, bytes_accessed=4 * 10**5)


def low_half(shape):
    return lax.broadcasted_iota(jnp.int32, shape, len(shape) - 1) < HEAD_DIM


def swap_halves(block):
    return pltpu.roll(block, HEAD_DIM, 1)


def layer_norm(wide):
    centre = jnp.mean(wide, axis=-1, keepdims=True)
    apart = wide - centre
    spread = jnp.mean(apart * apart, axis=-1, keepdims=True)
    return (apart * lax.rsqrt(spread + 1e-05)).astype(BF16)


def dot(left, right):
    return jnp.dot(left, right, preferred_element_type=F32)


def dot_t(left, right):
    return lax.dot_general(left, right, (((1,), (1,)), ((), ())), preferred_element_type=F32)


def packed_blocks(proj):
    rows, columns = proj.shape
    first = lax.broadcasted_iota(jnp.int32, (2 * LANES, LANES), 0) // HEAD_DIM % 2
    second = lax.broadcasted_iota(jnp.int32, (2 * LANES, LANES), 1) // HEAD_DIM
    group = jnp.where(first == second, 1.0 / HEAD_DIM, 0.0).astype(BF16)
    low = low_half((rows, LANES))
    parts = [proj[:, i * LANES : (i + 1) * LANES] for i in range(columns // LANES)]
    means = []
    for part in parts:
        square = part * part
        high = square.astype(BF16)
        rest = (square - high.astype(F32)).astype(BF16)
        means.append(dot(jnp.concatenate([high, rest], axis=1), group))
    blocks = []
    for i, (part, mean) in enumerate(zip(parts, means, strict=True)):
        factor = lax.rsqrt(mean + 1e-06)
        if i % 3 == 0:
            factor = jnp.where(low, factor * WEIGHT_SCALE, factor)
        elif i % 3 == 1:
            factor = jnp.where(low, 1.0, factor * WEIGHT_SCALE)
        else:
            factor = jnp.where(low, factor, 1.0)
        blocks.append(part * factor)
    return blocks


def send_tokens_kernel(tokens, out, rows):
    frames, patches, width = tokens.shape
    parts = width // LANES
    for f in range(frames):
        for c in range(parts):
            part = tokens[f, :, c * LANES : (c + 1) * LANES].astype(F32)
            rows[pl.ds(f * parts + c, patches, stride=frames * parts), :] = part
    out[...] = rows[...].reshape(out.shape).astype(BF16)


def time_kernel(tokens, weight, out, rows, sent):
    count, per, _ = tokens.shape
    width = weight.shape[0]
    parts = width // LANES
    span = count * per // parts
    rows[...] = tokens[...].astype(F32).reshape(rows.shape)
    wide = jnp.concatenate(
        [rows[pl.ds(c, span, stride=parts), :] for c in range(parts)], axis=1
    )
    blocks = packed_blocks(dot(layer_norm(wide), weight[...]))
    pairs = len(blocks) // 3
    low = low_half((span, LANES))
    high = jnp.logical_not(low)
    heads = []
    for j in range(pairs):
        first, middle, last = blocks[3 * j : 3 * j + 3]
        heads.append((low, first, middle))
        heads.append((high, jnp.where(low, last, middle), last))
    scores = [
        dot_t(jnp.where(keep, both, 0.0).astype(BF16), swap_halves(both).astype(BF16))
        for keep, both, _ in heads
    ]
    weights = [jnp.exp2(score).astype(BF16) for score in scores]
    summed = [
        dot(weight, jnp.where(keep, block, 1.0).astype(BF16))
        for weight, (keep, _, block) in zip(weights, heads, strict=True)
    ]
    for j in range(pairs):
        even, odd = summed[2 * j : 2 * j + 2]
        total = swap_halves(jnp.where(low, odd, even))
        sent[pl.ds(j, span, stride=pairs), :] = jnp.where(low, even, odd) / total
    out[...] = sent[...].reshape(out.shape).astype(BF16)


def middle_kernel(attended, tokens, time_output, space_input, out, hidden_out, rows):
    frames, patches, width = tokens.shape
    inner = time_output.shape[0]
    parts = inner // LANES
    rows[...] = attended[...].astype(F32).reshape(rows.shape)
    back = jnp.concatenate(
        [
            jnp.concatenate(
                [
                    rows[pl.ds(f * parts + c, patches, stride=frames * parts), :]
                    for c in range(parts)
                ],
                axis=1,
            )
            for f in range(frames)
        ],
        axis=0,
    ).astype(BF16)
    wide = tokens[...].astype(F32).reshape(frames * patches, width)
    hidden = (wide + dot(back, time_output[...])).astype(BF16)
    hidden_out[...] = hidden
    blocks = packed_blocks(dot(layer_norm(hidden.astype(F32)), space_input[...]))
    pairs = len(blocks) // 3
    low = low_half((frames * patches, LANES))
    low_few = low_half((patches // 2, LANES))
    for j in range(pairs):
        first, middle, last = blocks[3 * j : 3 * j + 3]
        mixed = swap_halves(jnp.where(low, last, middle))
        for odd, query_key, value in ((0, first, middle), (1, mixed, last)):
            turned = swap_halves(value)
            lower, upper = (turned, value) if odd else (value, turned)
            for f in range(frames):
                start, half = f * patches, f * patches + patches // 2
                at = f * 2 * pairs + 2 * j + odd
                out[at, :patches, :] = query_key[start : start + patches].astype(BF16)
                out[at, patches:, :] = jnp.where(
                    low_few, lower[start:half], upper[half : start + patches]
                ).astype(BF16)


def space_kernel(pair, out):
    count, rows, _ = pair.shape
    half = rows // 3
    patches = 2 * half
    span = count * patches
    low = low_half((span, LANES))
    query_key = pair[:, :patches, :].reshape(span, LANES)
    wide = query_key.astype(F32)
    query = jnp.where(low, wide, 0.0).astype(BF16)
    keys = swap_halves(wide).astype(BF16)
    values = pair[:, patches:, :].astype(F32).reshape(count * half, LANES)
    turned = swap_halves(values)
    value = jnp.concatenate(
        [values.reshape(count, half, LANES), turned.reshape(count, half, LANES)], axis=1
    ).reshape(span, LANES)
    value = jnp.where(low, value, 1.0).astype(BF16)
    half_span = span // 2
    scores = [dot_t(query[i : i + half_span], keys) for i in (0, half_span)]
    weights = [jnp.exp2(score).astype(BF16) for score in scores]
    summed = jnp.concatenate([dot(weight, value) for weight in weights], axis=0)
    done = summed / swap_halves(summed)
    other = swap_halves(done).reshape(count, patches, LANES)
    done = done.reshape(count, patches, LANES)
    low_few = low_half((count, half, LANES))
    out[...] = jnp.where(low_few, done[:, :half], other[:, half:]).astype(BF16)


def final_kernel(back, hidden, weight, out):
    count, half, _ = back.shape
    frames, patches, width = out.shape
    heads = count // frames
    low = low_half((half, LANES))
    frame_rows = []
    for f in range(frames):
        columns = []
        for j in range(heads // 2):
            even = back[f * heads + 2 * j].astype(F32)
            odd = back[f * heads + 2 * j + 1].astype(F32)
            lower = jnp.where(low, even, swap_halves(odd))
            upper = jnp.where(low, swap_halves(even), odd)
            columns.append(jnp.concatenate([lower, upper], axis=0))
        frame_rows.append(jnp.concatenate(columns, axis=1))
    attended = jnp.concatenate(frame_rows, axis=0).astype(BF16)
    final = hidden[...].astype(F32) + dot(attended, weight[...])
    out[...] = final.astype(BF16).reshape(out.shape)


def call(kernel, out_shape, scratch, *args, cost=None):
    return pl.pallas_call(
        kernel,
        out_shape=out_shape,
        in_specs=[pl.BlockSpec(memory_space=pltpu.VMEM)] * len(args),
        out_specs=jax.tree.map(lambda _: pl.BlockSpec(memory_space=pltpu.VMEM), out_shape),
        scratch_shapes=scratch,
        compiler_params=pltpu.CompilerParams(vmem_limit_bytes=12 * 2**20),
        cost_estimate=cost,
    )(*[pltpu.with_memory_space_constraint(arg, pltpu.VMEM) for arg in args])


def array(*shape):
    return pltpu.VMEM(shape, BF16)


def send_tokens(tokens):
    frames, patches, width = tokens.shape
    parts = width // LANES
    rows = pltpu.VMEM((frames * patches * parts, LANES), F32)
    return call(send_tokens_kernel, array(patches, frames * parts, LANES), [rows], tokens, cost=AHEAD)


def time_half(moved, time_input):
    count, per, _ = moved.shape
    span = count * per * LANES // time_input.shape[0]
    parts = time_input.shape[1] // 3 // LANES
    rows = pltpu.VMEM((count * per, LANES), F32)
    sent = pltpu.VMEM((span * parts, LANES), F32)
    shape = array(count, span * parts // count, LANES)
    return call(time_kernel, shape, [rows, sent], moved, time_input, cost=AHEAD)


def middle(returned, tokens, time_output, space_input):
    frames, patches, width = tokens.shape
    heads = time_output.shape[0] // HEAD_DIM
    count, per, _ = returned.shape
    rows = pltpu.VMEM((count * per, LANES), F32)
    shapes = (array(frames * heads, patches * 3 // 2, LANES), array(frames * patches, width))
    return call(middle_kernel, shapes, [rows], returned, tokens, time_output, space_input)


def space_half(pair):
    count, rows, _ = pair.shape
    return call(space_kernel, array(count, rows // 3, LANES), [], pair)


def final_half(back, hidden, space_output, shape):
    return call(final_kernel, jax.ShapeDtypeStruct(shape, BF16), [], back, hidden, space_output)


def exchange(messages, axis, order):
    return lax.all_to_all(messages, axis, 0, 0, tiled=True, axis_index_groups=[order])


def per_device(tokens, time_input, time_output, space_input, space_output):
    time_count = lax.axis_size("tm")
    time_order = [(TIME_FIRST + i) % time_count for i in range(time_count)]
    stripe_order = list(reversed(range(lax.axis_size("stripe"))))
    moved = exchange(send_tokens(tokens), "tm", time_order)
    attended = time_half(moved, time_input)
    returned = exchange(attended, "tm", time_order)
    packed, hidden = middle(returned, tokens, time_output, space_input)
    pair = exchange(packed, "stripe", stripe_order)
    back = exchange(space_half(pair), "stripe", stripe_order)
    return final_half(back, hidden, space_output, tokens.shape)


def solution(mesh):
    placed = (P("tm", "stripe", None), P(), P(), P(), P())
    return jax.shard_map(
        per_device, mesh=mesh, in_specs=placed, out_specs=P("tm", "stripe", None), check_vma=False
    )
```

```python
import math

import jax
import jax.numpy as jnp
from jax import lax
from jax.experimental import pallas as pl
from jax.experimental.pallas import tpu as pltpu
from jax.sharding import PartitionSpec as P

HEAD_DIM = 64
LANES = 128
F32 = jnp.float32
BF16 = jnp.bfloat16
WEIGHT_SCALE = 2.0 / math.sqrt(HEAD_DIM) * math.log2(math.e)

TIME_FIRST = 29
STRIPE_FIRST = 10
AHEAD = pl.CostEstimate(flops=5 * 10**9, transcendentals=0, bytes_accessed=4 * 10**5)


def low_half(shape):
    return lax.broadcasted_iota(jnp.int32, shape, len(shape) - 1) < HEAD_DIM


def swap_halves(block):
    return pltpu.roll(block, HEAD_DIM, 1)


def layer_norm(wide):
    centre = jnp.mean(wide, axis=-1, keepdims=True)
    apart = wide - centre
    spread = jnp.mean(apart * apart, axis=-1, keepdims=True)
    return (apart * lax.rsqrt(spread + 1e-05)).astype(BF16)


def dot(left, right):
    return jnp.dot(left, right, preferred_element_type=F32)


def dot_t(left, right):
    return lax.dot_general(left, right, (((1,), (1,)), ((), ())), preferred_element_type=F32)


def packed_blocks(proj):
    rows, columns = proj.shape
    first = lax.broadcasted_iota(jnp.int32, (2 * LANES, LANES), 0) // HEAD_DIM % 2
    second = lax.broadcasted_iota(jnp.int32, (2 * LANES, LANES), 1) // HEAD_DIM
    group = jnp.where(first == second, 1.0 / HEAD_DIM, 0.0).astype(BF16)
    low = low_half((rows, LANES))
    parts = [proj[:, i * LANES : (i + 1) * LANES] for i in range(columns // LANES)]
    means = []
    for part in parts:
        square = part * part
        high = square.astype(BF16)
        rest = (square - high.astype(F32)).astype(BF16)
        means.append(dot(jnp.concatenate([high, rest], axis=1), group))
    blocks = []
    for i, (part, mean) in enumerate(zip(parts, means, strict=True)):
        factor = lax.rsqrt(mean + 1e-06)
        if i % 3 == 0:
            factor = jnp.where(low, factor * WEIGHT_SCALE, factor)
        elif i % 3 == 1:
            factor = jnp.where(low, 1.0, factor * WEIGHT_SCALE)
        else:
            factor = jnp.where(low, factor, 1.0)
        blocks.append(part * factor)
    return blocks


def send_tokens_kernel(tokens, out, rows):
    frames, patches, width = tokens.shape
    parts = width // LANES
    for f in range(frames):
        for c in range(parts):
            part = tokens[f, :, c * LANES : (c + 1) * LANES].astype(F32)
            rows[pl.ds(f * parts + c, patches, stride=frames * parts), :] = part
    out[...] = rows[...].reshape(out.shape).astype(BF16)


def time_kernel(tokens, weight, out, rows, sent):
    count, per, _ = tokens.shape
    width = weight.shape[0]
    parts = width // LANES
    span = count * per // parts
    rows[...] = tokens[...].astype(F32).reshape(rows.shape)
    wide = jnp.concatenate(
        [rows[pl.ds(c, span, stride=parts), :] for c in range(parts)], axis=1
    )
    blocks = packed_blocks(dot(layer_norm(wide), weight[...]))
    pairs = len(blocks) // 3
    low = low_half((span, LANES))
    high = jnp.logical_not(low)
    heads = []
    for j in range(pairs):
        first, middle, last = blocks[3 * j : 3 * j + 3]
        heads.append((low, first, middle))
        heads.append((high, jnp.where(low, last, middle), last))
    scores = [
        dot_t(jnp.where(keep, both, 0.0).astype(BF16), swap_halves(both).astype(BF16))
        for keep, both, _ in heads
    ]
    weights = [jnp.exp2(score).astype(BF16) for score in scores]
    summed = [
        dot(weight, jnp.where(keep, block, 1.0).astype(BF16))
        for weight, (keep, _, block) in zip(weights, heads, strict=True)
    ]
    for j in range(pairs):
        even, odd = summed[2 * j : 2 * j + 2]
        total = swap_halves(jnp.where(low, odd, even))
        sent[pl.ds(j, span, stride=pairs), :] = jnp.where(low, even, odd) / total
    out[...] = sent[...].reshape(out.shape).astype(BF16)


def middle_kernel(attended, tokens, time_output, space_input, out, hidden_out, rows):
    frames, patches, width = tokens.shape
    inner = time_output.shape[0]
    parts = inner // LANES
    rows[...] = attended[...].astype(F32).reshape(rows.shape)
    back = jnp.concatenate(
        [
            jnp.concatenate(
                [
                    rows[pl.ds(f * parts + c, patches, stride=frames * parts), :]
                    for c in range(parts)
                ],
                axis=1,
            )
            for f in range(frames)
        ],
        axis=0,
    ).astype(BF16)
    wide = tokens[...].astype(F32).reshape(frames * patches, width)
    hidden = (wide + dot(back, time_output[...])).astype(BF16)
    hidden_out[...] = hidden
    blocks = packed_blocks(dot(layer_norm(hidden.astype(F32)), space_input[...]))
    pairs = len(blocks) // 3
    low = low_half((frames * patches, LANES))
    low_few = low_half((patches // 2, LANES))
    for j in range(pairs):
        first, middle, last = blocks[3 * j : 3 * j + 3]
        mixed = swap_halves(jnp.where(low, last, middle))
        for odd, query_key, value in ((0, first, middle), (1, mixed, last)):
            turned = swap_halves(value)
            lower, upper = (turned, value) if odd else (value, turned)
            for f in range(frames):
                start, half = f * patches, f * patches + patches // 2
                at = f * 2 * pairs + 2 * j + odd
                out[at, :patches, :] = query_key[start : start + patches].astype(BF16)
                out[at, patches:, :] = jnp.where(
                    low_few, lower[start:half], upper[half : start + patches]
                ).astype(BF16)


def space_kernel(pair, out):
    count, rows, _ = pair.shape
    half = rows // 3
    patches = 2 * half
    span = count * patches
    low = low_half((span, LANES))
    query_key = pair[:, :patches, :].reshape(span, LANES)
    wide = query_key.astype(F32)
    query = jnp.where(low, wide, 0.0).astype(BF16)
    keys = swap_halves(wide).astype(BF16)
    values = pair[:, patches:, :].astype(F32).reshape(count * half, LANES)
    turned = swap_halves(values)
    value = jnp.concatenate(
        [values.reshape(count, half, LANES), turned.reshape(count, half, LANES)], axis=1
    ).reshape(span, LANES)
    value = jnp.where(low, value, 1.0).astype(BF16)
    half_span = span // 2
    scores = [dot_t(query[i : i + half_span], keys) for i in (0, half_span)]
    weights = [jnp.exp2(score).astype(BF16) for score in scores]
    summed = jnp.concatenate([dot(weight, value) for weight in weights], axis=0)
    done = summed / swap_halves(summed)
    other = swap_halves(done).reshape(count, patches, LANES)
    done = done.reshape(count, patches, LANES)
    low_few = low_half((count, half, LANES))
    out[...] = jnp.where(low_few, done[:, :half], other[:, half:]).astype(BF16)


def final_kernel(back, hidden, weight, out):
    count, half, _ = back.shape
    frames, patches, width = out.shape
    heads = count // frames
    low = low_half((half, LANES))
    frame_rows = []
    for f in range(frames):
        columns = []
        for j in range(heads // 2):
            even = back[f * heads + 2 * j].astype(F32)
            odd = back[f * heads + 2 * j + 1].astype(F32)
            lower = jnp.where(low, even, swap_halves(odd))
            upper = jnp.where(low, swap_halves(even), odd)
            columns.append(jnp.concatenate([lower, upper], axis=0))
        frame_rows.append(jnp.concatenate(columns, axis=1))
    attended = jnp.concatenate(frame_rows, axis=0).astype(BF16)
    final = hidden[...].astype(F32) + dot(attended, weight[...])
    out[...] = final.astype(BF16).reshape(out.shape)


def call(kernel, out_shape, scratch, *args, cost=None):
    return pl.pallas_call(
        kernel,
        out_shape=out_shape,
        in_specs=[pl.BlockSpec(memory_space=pltpu.VMEM)] * len(args),
        out_specs=jax.tree.map(lambda _: pl.BlockSpec(memory_space=pltpu.VMEM), out_shape),
        scratch_shapes=scratch,
        compiler_params=pltpu.CompilerParams(vmem_limit_bytes=12 * 2**20),
        cost_estimate=cost,
    )(*[pltpu.with_memory_space_constraint(arg, pltpu.VMEM) for arg in args])


def array(*shape):
    return pltpu.VMEM(shape, BF16)


def send_tokens(tokens):
    frames, patches, width = tokens.shape
    parts = width // LANES
    rows = pltpu.VMEM((frames * patches * parts, LANES), F32)
    return call(send_tokens_kernel, array(patches, frames * parts, LANES), [rows], tokens, cost=AHEAD)


def time_half(moved, time_input):
    count, per, _ = moved.shape
    span = count * per * LANES // time_input.shape[0]
    parts = time_input.shape[1] // 3 // LANES
    rows = pltpu.VMEM((count * per, LANES), F32)
    sent = pltpu.VMEM((span * parts, LANES), F32)
    shape = array(count, span * parts // count, LANES)
    return call(time_kernel, shape, [rows, sent], moved, time_input, cost=AHEAD)


def middle(returned, tokens, time_output, space_input):
    frames, patches, width = tokens.shape
    heads = time_output.shape[0] // HEAD_DIM
    count, per, _ = returned.shape
    rows = pltpu.VMEM((count * per, LANES), F32)
    shapes = (array(frames * heads, patches * 3 // 2, LANES), array(frames * patches, width))
    return call(middle_kernel, shapes, [rows], returned, tokens, time_output, space_input)


def space_half(pair):
    count, rows, _ = pair.shape
    return call(space_kernel, array(count, rows // 3, LANES), [], pair)


def final_half(back, hidden, space_output, shape):
    return call(final_kernel, jax.ShapeDtypeStruct(shape, BF16), [], back, hidden, space_output)


def exchange(messages, axis, order):
    return lax.all_to_all(messages, axis, 0, 0, tiled=True, axis_index_groups=[order])


def per_device(tokens, time_input, time_output, space_input, space_output):
    time_count = lax.axis_size("tm")
    time_order = [(TIME_FIRST + i) % time_count for i in range(time_count)]
    others = [i for i in range(lax.axis_size("stripe")) if i != STRIPE_FIRST]
    stripe_order = [STRIPE_FIRST, *others]
    moved = exchange(send_tokens(tokens), "tm", time_order)
    attended = time_half(moved, time_input)
    returned = exchange(attended, "tm", time_order)
    packed, hidden = middle(returned, tokens, time_output, space_input)
    pair = exchange(packed, "stripe", stripe_order)
    back = exchange(space_half(pair), "stripe", stripe_order)
    return final_half(back, hidden, space_output, tokens.shape)


def solution(mesh):
    placed = (P("tm", "stripe", None), P(), P(), P(), P())
    return jax.shard_map(
        per_device, mesh=mesh, in_specs=placed, out_specs=P("tm", "stripe", None), check_vma=False
    )
```

```python
import math

import jax
import jax.numpy as jnp
from jax import lax
from jax.experimental import pallas as pl
from jax.experimental.pallas import tpu as pltpu
from jax.sharding import PartitionSpec as P

HEAD_DIM = 64
LANES = 128
F32 = jnp.float32
BF16 = jnp.bfloat16
WEIGHT_SCALE = 2.0 / math.sqrt(HEAD_DIM) * math.log2(math.e)

TIME_FIRST = 29
STRIPE_FIRST = 10
AHEAD = pl.CostEstimate(flops=5 * 10**9, transcendentals=0, bytes_accessed=4 * 10**5)


def low_half(shape):
    return lax.broadcasted_iota(jnp.int32, shape, len(shape) - 1) < HEAD_DIM


def swap_halves(block):
    return pltpu.roll(block, HEAD_DIM, 1)


def layer_norm(wide):
    centre = jnp.mean(wide, axis=-1, keepdims=True)
    apart = wide - centre
    spread = jnp.mean(apart * apart, axis=-1, keepdims=True)
    return (apart * lax.rsqrt(spread + 1e-05)).astype(BF16)


def dot(left, right):
    return jnp.dot(left, right, preferred_element_type=F32)


def dot_t(left, right):
    return lax.dot_general(left, right, (((1,), (1,)), ((), ())), preferred_element_type=F32)


def packed_blocks(proj):
    rows, columns = proj.shape
    first = lax.broadcasted_iota(jnp.int32, (2 * LANES, LANES), 0) // HEAD_DIM % 2
    second = lax.broadcasted_iota(jnp.int32, (2 * LANES, LANES), 1) // HEAD_DIM
    group = jnp.where(first == second, 1.0 / HEAD_DIM, 0.0).astype(BF16)
    low = low_half((rows, LANES))
    parts = [proj[:, i * LANES : (i + 1) * LANES] for i in range(columns // LANES)]
    means = []
    for part in parts:
        square = part * part
        high = square.astype(BF16)
        rest = (square - high.astype(F32)).astype(BF16)
        means.append(dot(jnp.concatenate([high, rest], axis=1), group))
    blocks = []
    for i, (part, mean) in enumerate(zip(parts, means, strict=True)):
        factor = lax.rsqrt(mean + 1e-06)
        if i % 3 == 0:
            factor = jnp.where(low, factor * WEIGHT_SCALE, factor)
        elif i % 3 == 1:
            factor = jnp.where(low, 1.0, factor * WEIGHT_SCALE)
        else:
            factor = jnp.where(low, factor, 1.0)
        blocks.append(part * factor)
    return blocks


def send_tokens_kernel(tokens, out, rows):
    frames, patches, width = tokens.shape
    parts = width // LANES
    for f in range(frames):
        for c in range(parts):
            part = tokens[f, :, c * LANES : (c + 1) * LANES].astype(F32)
            rows[pl.ds(f * parts + c, patches, stride=frames * parts), :] = part
    out[...] = rows[...].reshape(out.shape).astype(BF16)


def time_kernel(tokens, weight, out, rows, sent):
    count, per, _ = tokens.shape
    width = weight.shape[0]
    parts = width // LANES
    span = count * per // parts
    rows[...] = tokens[...].astype(F32).reshape(rows.shape)
    wide = jnp.concatenate(
        [rows[pl.ds(c, span, stride=parts), :] for c in range(parts)], axis=1
    )
    blocks = packed_blocks(dot(layer_norm(wide), weight[...]))
    pairs = len(blocks) // 3
    low = low_half((span, LANES))
    high = jnp.logical_not(low)
    heads = []
    for j in range(pairs):
        first, middle, last = blocks[3 * j : 3 * j + 3]
        heads.append((low, first, middle))
        heads.append((high, jnp.where(low, last, middle), last))
    scores = [
        dot_t(jnp.where(keep, both, 0.0).astype(BF16), swap_halves(both).astype(BF16))
        for keep, both, _ in heads
    ]
    weights = [jnp.exp2(score).astype(BF16) for score in scores]
    summed = [
        dot(weight, jnp.where(keep, block, 1.0).astype(BF16))
        for weight, (keep, _, block) in zip(weights, heads, strict=True)
    ]
    for j in range(pairs):
        even, odd = summed[2 * j : 2 * j + 2]
        total = swap_halves(jnp.where(low, odd, even))
        sent[pl.ds(j, span, stride=pairs), :] = jnp.where(low, even, odd) / total
    out[...] = sent[...].reshape(out.shape).astype(BF16)


def middle_kernel(attended, tokens, time_output, space_input, out, hidden_out, rows):
    frames, patches, width = tokens.shape
    inner = time_output.shape[0]
    parts = inner // LANES
    rows[...] = attended[...].astype(F32).reshape(rows.shape)
    back = jnp.concatenate(
        [
            jnp.concatenate(
                [
                    rows[pl.ds(f * parts + c, patches, stride=frames * parts), :]
                    for c in range(parts)
                ],
                axis=1,
            )
            for f in range(frames)
        ],
        axis=0,
    ).astype(BF16)
    wide = tokens[...].astype(F32).reshape(frames * patches, width)
    hidden = (wide + dot(back, time_output[...])).astype(BF16)
    hidden_out[...] = hidden
    blocks = packed_blocks(dot(layer_norm(hidden.astype(F32)), space_input[...]))
    pairs = len(blocks) // 3
    low = low_half((frames * patches, LANES))
    low_few = low_half((patches // 2, LANES))
    for j in range(pairs):
        first, middle, last = blocks[3 * j : 3 * j + 3]
        mixed = swap_halves(jnp.where(low, last, middle))
        for odd, query_key, value in ((0, first, middle), (1, mixed, last)):
            turned = swap_halves(value)
            lower, upper = (turned, value) if odd else (value, turned)
            for f in range(frames):
                start, half = f * patches, f * patches + patches // 2
                at = f * 2 * pairs + 2 * j + odd
                out[at, :patches, :] = query_key[start : start + patches].astype(BF16)
                out[at, patches:, :] = jnp.where(
                    low_few, lower[start:half], upper[half : start + patches]
                ).astype(BF16)


def space_kernel(pair, out):
    count, rows, _ = pair.shape
    half = rows // 3
    patches = 2 * half
    span = count * patches
    low = low_half((span, LANES))
    query_key = pair[:, :patches, :].reshape(span, LANES)
    wide = query_key.astype(F32)
    query = jnp.where(low, wide, 0.0).astype(BF16)
    keys = swap_halves(wide).astype(BF16)
    values = pair[:, patches:, :].astype(F32).reshape(count * half, LANES)
    turned = swap_halves(values)
    value = jnp.concatenate(
        [values.reshape(count, half, LANES), turned.reshape(count, half, LANES)], axis=1
    ).reshape(span, LANES)
    value = jnp.where(low, value, 1.0).astype(BF16)
    half_span = span // 2
    scores = [dot_t(query[i : i + half_span], keys) for i in (0, half_span)]
    weights = [jnp.exp2(score).astype(BF16) for score in scores]
    summed = jnp.concatenate([dot(weight, value) for weight in weights], axis=0)
    done = summed / swap_halves(summed)
    other = swap_halves(done).reshape(count, patches, LANES)
    done = done.reshape(count, patches, LANES)
    low_few = low_half((count, half, LANES))
    messages = jnp.where(low_few, done[:, :half], other[:, half:]).astype(BF16)
    out[...] = messages
    out[0] = messages[STRIPE_FIRST]
    out[STRIPE_FIRST] = messages[0]


def traded(place):
    return {0: STRIPE_FIRST, STRIPE_FIRST: 0}.get(place, place)


def final_kernel(back, hidden, weight, out):
    count, half, _ = back.shape
    frames, patches, width = out.shape
    heads = count // frames
    low = low_half((half, LANES))
    frame_rows = []
    for f in range(frames):
        columns = []
        for j in range(heads // 2):
            even = back[traded(f * heads + 2 * j)].astype(F32)
            odd = back[traded(f * heads + 2 * j + 1)].astype(F32)
            lower = jnp.where(low, even, swap_halves(odd))
            upper = jnp.where(low, swap_halves(even), odd)
            columns.append(jnp.concatenate([lower, upper], axis=0))
        frame_rows.append(jnp.concatenate(columns, axis=1))
    attended = jnp.concatenate(frame_rows, axis=0).astype(BF16)
    final = hidden[...].astype(F32) + dot(attended, weight[...])
    out[...] = final.astype(BF16).reshape(out.shape)


def call(kernel, out_shape, scratch, *args, cost=None):
    return pl.pallas_call(
        kernel,
        out_shape=out_shape,
        in_specs=[pl.BlockSpec(memory_space=pltpu.VMEM)] * len(args),
        out_specs=jax.tree.map(lambda _: pl.BlockSpec(memory_space=pltpu.VMEM), out_shape),
        scratch_shapes=scratch,
        compiler_params=pltpu.CompilerParams(vmem_limit_bytes=12 * 2**20),
        cost_estimate=cost,
    )(*[pltpu.with_memory_space_constraint(arg, pltpu.VMEM) for arg in args])


def array(*shape):
    return pltpu.VMEM(shape, BF16)


def send_tokens(tokens):
    frames, patches, width = tokens.shape
    parts = width // LANES
    rows = pltpu.VMEM((frames * patches * parts, LANES), F32)
    return call(send_tokens_kernel, array(patches, frames * parts, LANES), [rows], tokens, cost=AHEAD)


def time_half(moved, time_input):
    count, per, _ = moved.shape
    span = count * per * LANES // time_input.shape[0]
    parts = time_input.shape[1] // 3 // LANES
    rows = pltpu.VMEM((count * per, LANES), F32)
    sent = pltpu.VMEM((span * parts, LANES), F32)
    shape = array(count, span * parts // count, LANES)
    return call(time_kernel, shape, [rows, sent], moved, time_input, cost=AHEAD)


def middle(returned, tokens, time_output, space_input):
    frames, patches, width = tokens.shape
    heads = time_output.shape[0] // HEAD_DIM
    count, per, _ = returned.shape
    rows = pltpu.VMEM((count * per, LANES), F32)
    shapes = (array(frames * heads, patches * 3 // 2, LANES), array(frames * patches, width))
    return call(middle_kernel, shapes, [rows], returned, tokens, time_output, space_input)


def space_half(pair):
    count, rows, _ = pair.shape
    return call(space_kernel, array(count, rows // 3, LANES), [], pair)


def final_half(back, hidden, space_output, shape):
    return call(final_kernel, jax.ShapeDtypeStruct(shape, BF16), [], back, hidden, space_output)


def exchange(messages, axis, order):
    return lax.all_to_all(messages, axis, 0, 0, tiled=True, axis_index_groups=[order])


def per_device(tokens, time_input, time_output, space_input, space_output):
    time_count = lax.axis_size("tm")
    time_order = [(TIME_FIRST + i) % time_count for i in range(time_count)]
    stripe_order, back_order = (
        [first, *(i for i in range(lax.axis_size("stripe")) if i != first)]
        for first in (STRIPE_FIRST, STRIPE_FIRST - 1)
    )
    moved = exchange(send_tokens(tokens), "tm", time_order)
    attended = time_half(moved, time_input)
    returned = exchange(attended, "tm", time_order)
    packed, hidden = middle(returned, tokens, time_output, space_input)
    pair = exchange(packed, "stripe", stripe_order)
    back = exchange(space_half(pair), "stripe", back_order)
    return final_half(back, hidden, space_output, tokens.shape)


def solution(mesh):
    placed = (P("tm", "stripe", None), P(), P(), P(), P())
    return jax.shard_map(
        per_device, mesh=mesh, in_specs=placed, out_specs=P("tm", "stripe", None), check_vma=False
    )
```

```python
import math

import jax
import jax.numpy as jnp
from jax import lax
from jax.experimental import pallas as pl
from jax.experimental.pallas import tpu as pltpu
from jax.sharding import PartitionSpec as P

HEAD_DIM = 64
LANES = 128
F32 = jnp.float32
BF16 = jnp.bfloat16
WEIGHT_SCALE = 2.0 / math.sqrt(HEAD_DIM) * math.log2(math.e)

TIME_FIRST = 29
STRIPE_FIRST = 10
BACK_FIRST = 14
AHEAD = pl.CostEstimate(flops=5 * 10**9, transcendentals=0, bytes_accessed=4 * 10**5)


def low_half(shape):
    return lax.broadcasted_iota(jnp.int32, shape, len(shape) - 1) < HEAD_DIM


def swap_halves(block):
    return pltpu.roll(block, HEAD_DIM, 1)


def layer_norm(wide):
    centre = jnp.mean(wide, axis=-1, keepdims=True)
    apart = wide - centre
    spread = jnp.mean(apart * apart, axis=-1, keepdims=True)
    return (apart * lax.rsqrt(spread + 1e-05)).astype(BF16)


def dot(left, right):
    return jnp.dot(left, right, preferred_element_type=F32)


def dot_t(left, right):
    return lax.dot_general(left, right, (((1,), (1,)), ((), ())), preferred_element_type=F32)


def packed_blocks(proj):
    rows, columns = proj.shape
    first = lax.broadcasted_iota(jnp.int32, (2 * LANES, LANES), 0) // HEAD_DIM % 2
    second = lax.broadcasted_iota(jnp.int32, (2 * LANES, LANES), 1) // HEAD_DIM
    group = jnp.where(first == second, 1.0 / HEAD_DIM, 0.0).astype(BF16)
    low = low_half((rows, LANES))
    parts = [proj[:, i * LANES : (i + 1) * LANES] for i in range(columns // LANES)]
    means = []
    for part in parts:
        square = part * part
        high = square.astype(BF16)
        rest = (square - high.astype(F32)).astype(BF16)
        means.append(dot(jnp.concatenate([high, rest], axis=1), group))
    blocks = []
    for i, (part, mean) in enumerate(zip(parts, means, strict=True)):
        factor = lax.rsqrt(mean + 1e-06)
        if i % 3 == 0:
            factor = jnp.where(low, factor * WEIGHT_SCALE, factor)
        elif i % 3 == 1:
            factor = jnp.where(low, 1.0, factor * WEIGHT_SCALE)
        else:
            factor = jnp.where(low, factor, 1.0)
        blocks.append(part * factor)
    return blocks


def send_tokens_kernel(tokens, out, rows):
    frames, patches, width = tokens.shape
    parts = width // LANES
    for f in range(frames):
        for c in range(parts):
            part = tokens[f, :, c * LANES : (c + 1) * LANES].astype(F32)
            rows[pl.ds(f * parts + c, patches, stride=frames * parts), :] = part
    out[...] = rows[...].reshape(out.shape).astype(BF16)


def time_kernel(tokens, weight, out, rows, sent):
    count, per, _ = tokens.shape
    width = weight.shape[0]
    parts = width // LANES
    span = count * per // parts
    rows[...] = tokens[...].astype(F32).reshape(rows.shape)
    wide = jnp.concatenate(
        [rows[pl.ds(c, span, stride=parts), :] for c in range(parts)], axis=1
    )
    blocks = packed_blocks(dot(layer_norm(wide), weight[...]))
    pairs = len(blocks) // 3
    low = low_half((span, LANES))
    high = jnp.logical_not(low)
    heads = []
    for j in range(pairs):
        first, middle, last = blocks[3 * j : 3 * j + 3]
        heads.append((low, first, middle))
        heads.append((high, jnp.where(low, last, middle), last))
    scores = [
        dot_t(jnp.where(keep, both, 0.0).astype(BF16), swap_halves(both).astype(BF16))
        for keep, both, _ in heads
    ]
    weights = [jnp.exp2(score).astype(BF16) for score in scores]
    summed = [
        dot(weight, jnp.where(keep, block, 1.0).astype(BF16))
        for weight, (keep, _, block) in zip(weights, heads, strict=True)
    ]
    for j in range(pairs):
        even, odd = summed[2 * j : 2 * j + 2]
        total = swap_halves(jnp.where(low, odd, even))
        sent[pl.ds(j, span, stride=pairs), :] = jnp.where(low, even, odd) / total
    out[...] = sent[...].reshape(out.shape).astype(BF16)


def middle_kernel(attended, tokens, time_output, space_input, out, hidden_out, rows):
    frames, patches, width = tokens.shape
    inner = time_output.shape[0]
    parts = inner // LANES
    rows[...] = attended[...].astype(F32).reshape(rows.shape)
    back = jnp.concatenate(
        [
            jnp.concatenate(
                [
                    rows[pl.ds(f * parts + c, patches, stride=frames * parts), :]
                    for c in range(parts)
                ],
                axis=1,
            )
            for f in range(frames)
        ],
        axis=0,
    ).astype(BF16)
    wide = tokens[...].astype(F32).reshape(frames * patches, width)
    hidden = (wide + dot(back, time_output[...])).astype(BF16)
    hidden_out[...] = hidden
    blocks = packed_blocks(dot(layer_norm(hidden.astype(F32)), space_input[...]))
    pairs = len(blocks) // 3
    low = low_half((frames * patches, LANES))
    low_few = low_half((patches // 2, LANES))
    for j in range(pairs):
        first, middle, last = blocks[3 * j : 3 * j + 3]
        mixed = swap_halves(jnp.where(low, last, middle))
        for odd, query_key, value in ((0, first, middle), (1, mixed, last)):
            turned = swap_halves(value)
            lower, upper = (turned, value) if odd else (value, turned)
            for f in range(frames):
                start, half = f * patches, f * patches + patches // 2
                at = f * 2 * pairs + 2 * j + odd
                out[at, :patches, :] = query_key[start : start + patches].astype(BF16)
                out[at, patches:, :] = jnp.where(
                    low_few, lower[start:half], upper[half : start + patches]
                ).astype(BF16)


def space_kernel(pair, out):
    count, rows, _ = pair.shape
    half = rows // 3
    patches = 2 * half
    span = count * patches
    low = low_half((span, LANES))
    query_key = pair[:, :patches, :].reshape(span, LANES)
    wide = query_key.astype(F32)
    query = jnp.where(low, wide, 0.0).astype(BF16)
    keys = swap_halves(wide).astype(BF16)
    values = pair[:, patches:, :].astype(F32).reshape(count * half, LANES)
    turned = swap_halves(values)
    value = jnp.concatenate(
        [values.reshape(count, half, LANES), turned.reshape(count, half, LANES)], axis=1
    ).reshape(span, LANES)
    value = jnp.where(low, value, 1.0).astype(BF16)
    half_span = span // 2
    scores = [dot_t(query[i : i + half_span], keys) for i in (0, half_span)]
    weights = [jnp.exp2(score).astype(BF16) for score in scores]
    summed = jnp.concatenate([dot(weight, value) for weight in weights], axis=0)
    done = summed / swap_halves(summed)
    other = swap_halves(done).reshape(count, patches, LANES)
    done = done.reshape(count, patches, LANES)
    low_few = low_half((count, half, LANES))
    messages = jnp.where(low_few, done[:, :half], other[:, half:]).astype(BF16)
    out[...] = messages
    out[0] = messages[BACK_FIRST]
    out[BACK_FIRST] = messages[0]


def traded(place):
    return {0: BACK_FIRST, BACK_FIRST: 0}.get(place, place)


def final_kernel(back, hidden, weight, out):
    count, half, _ = back.shape
    frames, patches, width = out.shape
    heads = count // frames
    low = low_half((half, LANES))
    frame_rows = []
    for f in range(frames):
        columns = []
        for j in range(heads // 2):
            even = back[traded(f * heads + 2 * j)].astype(F32)
            odd = back[traded(f * heads + 2 * j + 1)].astype(F32)
            lower = jnp.where(low, even, swap_halves(odd))
            upper = jnp.where(low, swap_halves(even), odd)
            columns.append(jnp.concatenate([lower, upper], axis=0))
        frame_rows.append(jnp.concatenate(columns, axis=1))
    attended = jnp.concatenate(frame_rows, axis=0).astype(BF16)
    final = hidden[...].astype(F32) + dot(attended, weight[...])
    out[...] = final.astype(BF16).reshape(out.shape)


def call(kernel, out_shape, scratch, *args, cost=None):
    return pl.pallas_call(
        kernel,
        out_shape=out_shape,
        in_specs=[pl.BlockSpec(memory_space=pltpu.VMEM)] * len(args),
        out_specs=jax.tree.map(lambda _: pl.BlockSpec(memory_space=pltpu.VMEM), out_shape),
        scratch_shapes=scratch,
        compiler_params=pltpu.CompilerParams(vmem_limit_bytes=12 * 2**20),
        cost_estimate=cost,
    )(*[pltpu.with_memory_space_constraint(arg, pltpu.VMEM) for arg in args])


def array(*shape):
    return pltpu.VMEM(shape, BF16)


def send_tokens(tokens):
    frames, patches, width = tokens.shape
    parts = width // LANES
    rows = pltpu.VMEM((frames * patches * parts, LANES), F32)
    return call(send_tokens_kernel, array(patches, frames * parts, LANES), [rows], tokens, cost=AHEAD)


def time_half(moved, time_input):
    count, per, _ = moved.shape
    span = count * per * LANES // time_input.shape[0]
    parts = time_input.shape[1] // 3 // LANES
    rows = pltpu.VMEM((count * per, LANES), F32)
    sent = pltpu.VMEM((span * parts, LANES), F32)
    shape = array(count, span * parts // count, LANES)
    return call(time_kernel, shape, [rows, sent], moved, time_input, cost=AHEAD)


def middle(returned, tokens, time_output, space_input):
    frames, patches, width = tokens.shape
    heads = time_output.shape[0] // HEAD_DIM
    count, per, _ = returned.shape
    rows = pltpu.VMEM((count * per, LANES), F32)
    shapes = (array(frames * heads, patches * 3 // 2, LANES), array(frames * patches, width))
    return call(middle_kernel, shapes, [rows], returned, tokens, time_output, space_input)


def space_half(pair):
    count, rows, _ = pair.shape
    return call(space_kernel, array(count, rows // 3, LANES), [], pair)


def final_half(back, hidden, space_output, shape):
    return call(final_kernel, jax.ShapeDtypeStruct(shape, BF16), [], back, hidden, space_output)


def exchange(messages, axis, order):
    return lax.all_to_all(messages, axis, 0, 0, tiled=True, axis_index_groups=[order])


def per_device(tokens, time_input, time_output, space_input, space_output):
    time_count = lax.axis_size("tm")
    time_order = [(TIME_FIRST + i) % time_count for i in range(time_count)]
    others = [i for i in range(lax.axis_size("stripe")) if i != STRIPE_FIRST]
    stripe_order = [STRIPE_FIRST, *others]
    back_order = [stripe_order[traded(i)] for i in range(len(stripe_order))]
    moved = exchange(send_tokens(tokens), "tm", time_order)
    attended = time_half(moved, time_input)
    returned = exchange(attended, "tm", time_order)
    packed, hidden = middle(returned, tokens, time_output, space_input)
    pair = exchange(packed, "stripe", stripe_order)
    back = exchange(space_half(pair), "stripe", back_order)
    return final_half(back, hidden, space_output, tokens.shape)


def solution(mesh):
    placed = (P("tm", "stripe", None), P(), P(), P(), P())
    return jax.shard_map(
        per_device, mesh=mesh, in_specs=placed, out_specs=P("tm", "stripe", None), check_vma=False
    )
```
